32 devices in a mesh: groups: 2 (over y), seq: 4 (over z), head: 2 (over x), batch: 2 (over core).
Axes of the slice: x: 2, y: 2, z: 4, core: 2. Of those that a mesh axis runs over, the one named last changes fastest.
Arguments:
- query_rows: bfloat16 [4, 2048, 4096], P(('groups', 'batch'), 'seq', 'head'), parts along dimension 0, may hold values from -6 to 6
- key_rows: bfloat16 [4, 2048, 4096], P(('groups', 'batch'), 'seq', 'head'), parts along dimension 0, may hold values from -0.5 to 0.5
- value_rows: bfloat16 [4, 2048, 4096], P(('groups', 'batch'), 'seq', 'head'), parts along dimension 0, may hold values from -45 to 45
- coef_at: int32 [32], P('groups'), parts along dimension 0, may hold values from 0 to 2047, as said below
- coef_table: float32 [32, 6, 32], P('groups', None, 'head'), parts along dimension 0, may hold values from 0.1 to 1
- out_gain: float32 [4096], P('head'), may hold values from 0.5 to 1.5
Outputs:
- attended: bfloat16 [4, 2048, 4096], P(('groups', 'batch'), 'seq', 'head'), parts along dimension 0
The draws below stay inside these ranges and needn't reach their ends.
There are 2 independent parts, one for each index of `groups`. The reference program is written for one: setup_inputs(seed, part) draws one part's arguments, and reference() takes and returns one part's arrays. A program takes and returns all parts, laid end to end along the dimension named above; an argument that names none is the same for every part. Nothing has to cross between parts.
Inputs may be any that keep to these rules, and one draw needn't show every extreme that they name: `coef_at`: strictly increasing; the first is 0, the last is 2047, and each aligned stretch of 128 positions holds exactly one.
All inputs are finite; a program needn't handle non-finite values.
Results may differ from the reference program's by a relative error of at most 0.0053.
Values may be sent and summed in bfloat16 or wider, within the bound.
A program may use at most 64 MiB of HBM per device.

```python
import math
import jax
import jax.numpy as jnp
from jax import lax

HEADS = 32
HD = 128
TOK_DEV = 512
LOCAL_BITS = 3
BATCH = 2
TOKENS = 2048
SEQ_BITS = 2
LEVELS = 6
POINTS = 16
N_SEQ = 4


def draw_value_rows(key, part):
    width = HEADS * HD
    first, second = jax.random.split(jax.random.fold_in(key, 7), 2)
    column = jnp.exp(jax.random.uniform(second, (width,), jnp.float32, 0.0, math.log(10.0)))
    rising = jnp.exp(math.log(3.0) * jnp.arange(width, dtype=jnp.float32) / width)
    base = jax.random.normal(first, (BATCH, TOKENS, width), jnp.float32)
    base = jnp.clip(base, -6.0, 6.0)
    return (base * column * rising / 4.0).astype(jnp.bfloat16)


def draw_coef_at(key, part):
    stretch = TOKENS // POINTS
    offsets = jax.random.randint(jax.random.fold_in(key, 11), (POINTS,), 0, stretch)
    places = jnp.arange(POINTS, dtype=jnp.int32)
    inner = jnp.where(places == 0, 0, places * stretch + offsets)
    return jnp.where(places == POINTS - 1, TOKENS - 1, inner).astype(jnp.int32)


def block_levels(rng, dims, cuts, least, largest):
    level, own = 1.0, jax.random.fold_in(rng, 6)
    for dim, parts in cuts:
        heights = jnp.exp(jax.random.uniform(jax.random.fold_in(own, dim), (parts,), jnp.float32, least / len(cuts), largest / len(cuts)))
        level = level * jnp.repeat(heights, dims[dim] // parts).reshape([-1 if axis == dim else 1 for axis in range(len(dims))])
    return level


def gaussian(key, dims, spread, limit, pieces=(), held_as=jnp.bfloat16):
    loudness = block_levels(key, dims, pieces, -0.22, 0.18) if pieces else 1.0
    values = jax.random.normal(key, dims, jnp.float32) * spread * loudness
    return jnp.minimum(jnp.maximum(values, -limit), limit).astype(held_as)


def setup_inputs(seed: int = 0, part: int = 0) -> dict:
    arg_keys = jax.random.split(jax.random.key(seed), 7)
    part_splits = jax.random.split(jax.random.fold_in(arg_keys[6], part), 7)
    return {
        "query_rows": gaussian(part_splits[0], (BATCH, TOKENS, HEADS * HD), 1.0, 6.0, ((0, 2), (1, 4), (2, 2))),
        "key_rows": gaussian(part_splits[1], (BATCH, TOKENS, HEADS * HD), (HD ** -0.5), 0.5, ((0, 2), (1, 4), (2, 2))),
        "value_rows": draw_value_rows(jax.random.fold_in(jax.random.fold_in(arg_keys[6], part), 71), part),
        "coef_at": draw_coef_at(jax.random.fold_in(jax.random.fold_in(arg_keys[6], part), 71), part),
        "coef_table": jnp.clip(jnp.exp(math.log(1.0) - 2.3025851 * jax.random.uniform(part_splits[4], (POINTS, LEVELS, HEADS), jnp.float32) ** block_levels(part_splits[4], (POINTS, LEVELS, HEADS), ((2, 2),), -0.2, 0.2)), 0.1, 1.0),
        "out_gain": jnp.clip(1.0 + 0.1 * jax.random.normal(arg_keys[5], (HEADS * HD,), jnp.float32), 0.5, 1.5),
    }


EPSILON = 1e-06
HIGH = lax.Precision.HIGHEST

def span_levels(tokens_here):
    span_len = tokens_here // 2 ** LOCAL_BITS
    places = jnp.arange(tokens_here, dtype=jnp.int32)
    span_id = places // span_len
    same_span = (span_id[:, None] == span_id[None, :]) & (places[None, :] <= places[:, None])
    earlier = span_id[None, :] < span_id[:, None]
    differ = jnp.bitwise_xor(span_id[:, None], span_id[None, :])
    planes = [same_span] + [earlier & (jnp.right_shift(differ, level) == 1) for level in range(LOCAL_BITS)]
    return jnp.stack(planes).astype(jnp.float32)

def level_select(shard, sources, seq_bits):
    differ = jnp.bitwise_xor(shard, sources)
    earlier = sources < shard
    planes = [earlier & (jnp.right_shift(differ, level) == 1) for level in range(seq_bits)]
    return jnp.stack(planes).astype(jnp.float32)

def reference(query_rows, key_rows, value_rows, coef_at, coef_table, out_gain):
    shape5 = (BATCH, N_SEQ, TOK_DEV, HEADS, HD)

    def split(rows):
        return jnp.transpose(rows.reshape(shape5), (1, 0, 2, 3, 4))
    queries5 = split(query_rows)
    keys5 = split(key_rows)
    values5 = split(value_rows)
    states = jnp.einsum('pnshd,pnshe->pnhde', keys5.astype(jnp.float32), values5.astype(jnp.float32))
    states32 = states.astype(jnp.bfloat16).astype(jnp.float32)
    places = jnp.arange(TOKENS, dtype=jnp.int32)
    row_index = lax.optimization_barrier(jnp.sum((coef_at[None, :] <= places[:, None]).astype(jnp.int32), axis=1)) - 1
    weights = coef_table[row_index].reshape(N_SEQ, TOK_DEV, LEVELS, HEADS)
    masks = span_levels(TOK_DEV)
    local_count = LOCAL_BITS + 1

    def one_shard(inputs):
        shard, queries4, keys4, values4, shard_weights = inputs
        pair_weight = jnp.einsum('lts,tlh->hts', masks, shard_weights[:, :local_count, :], precision=HIGH)
        scores = jnp.einsum('nthd,nshd->nhts', queries4.astype(jnp.float32), keys4.astype(jnp.float32))
        probs = (scores * pair_weight[None]).astype(jnp.bfloat16)
        near = jnp.einsum('nhts,nshd->nthd', probs.astype(jnp.float32), values4.astype(jnp.float32))
        sources = jnp.arange(N_SEQ, dtype=jnp.int32)
        select = level_select(shard, sources, SEQ_BITS)
        buckets = jnp.einsum('lr,rnhde->lnhde', select, states32, precision=HIGH).astype(jnp.bfloat16)
        far_levels = jnp.einsum('nthd,lnhde->lnthe', queries4.astype(jnp.float32), buckets.astype(jnp.float32))
        far_weight = jnp.transpose(shard_weights[:, local_count:, :], (1, 0, 2))
        far = lax.optimization_barrier(jnp.sum(far_levels * far_weight[:, None, :, :, None], axis=0))
        return near + far
    mixed = lax.map(one_shard, (jnp.arange(N_SEQ, dtype=jnp.int32), queries5, keys5, values5, weights))
    mixed = jnp.transpose(mixed, (1, 0, 2, 3, 4)).reshape(BATCH, TOKENS, HEADS * HD)
    square = lax.optimization_barrier(jnp.sum(mixed * mixed, axis=2))
    scale = lax.rsqrt(square / (HEADS * HD) + EPSILON)
    return (mixed * scale[:, :, None] * out_gain).astype(jnp.bfloat16)
```

```python
import functools

import jax
import jax.numpy as jnp
from jax import lax
from jax.experimental import pallas as pl
from jax.experimental.pallas import tpu as pltpu
from jax.sharding import PartitionSpec as P

HEADS = 32
HD = 128
LOCAL_BITS = 3
EPSILON = 1e-06
HIGH = lax.Precision.HIGHEST
MESH = pl.DeviceIdType.MESH
LANES = 128
LEAD = 3
PIECES = 8
LATE = 2

ROWS_ROWS = (((0,), (0,)), ((), ()))
COLS_COLS = (((1,), (1,)), ((), ()))


def chunk_heads(heads):
    rest = heads - LATE
    pairs = (rest - 4) // 2
    sizes = [1] * LATE + [1, 1] + [2] * pairs + [1] * (rest - 2 - 2 * pairs)
    return [range(sum(sizes[:c]), sum(sizes[: c + 1])) for c in range(len(sizes))]


def dot(a, b, dims=(((1,), (0,)), ((), ())), precision=None):
    return lax.dot_general(a, b, dims, preferred_element_type=jnp.float32, precision=precision)


def kernel(
    n_seq, n_head,
    q_hbm, k_hbm, v_hbm, at_hbm, table_hbm, gain_hbm, mixed, scale_ref,
    q_s, k_s, v_s, at_ref, table_ref, gain_ref, state, first, buckets, table_s, lam_s, square_s, part_s, parts_in,
    near_s, ask_q, ask_near, lam_next, reply_s, reply_in,
    load_sem, small_sem, up_send, pass_send, recv_sem, part_send, part_recv,
    ask_send, ask_recv, reply_send, reply_recv,
):
    tokens, width = q_s.shape
    levels, heads = table_ref.shape[0], table_ref.shape[2]
    bits = levels - LOCAL_BITS - 1
    points = at_ref.shape[1]
    chunks = chunk_heads(heads)
    count = len(chunks)
    half, quarter = tokens // 2, tokens // 4
    span = tokens // 2**LOCAL_BITS
    me = lax.axis_index("seq")
    hx = lax.axis_index("head")
    has_next = me < n_seq - 1
    is_last = me == n_seq - 1
    helps = me == n_seq - 2
    following = {"seq": lax.rem(me + 1, n_seq)}
    before = {"seq": lax.rem(me + n_seq - 1, n_seq)}
    late = range(LATE)
    order = [*range(LATE, count), *late]
    partners = [{"head": lax.rem(hx + j, n_head)} for j in range(1, n_head)]

    barrier = pltpu.get_barrier_semaphore()

    @pl.when(me > 0)
    def _():
        pl.semaphore_signal(barrier, inc=1, device_id=before, device_id_type=MESH)

    @pl.when(helps)
    def _():
        pl.semaphore_signal(barrier, inc=1, device_id=following, device_id_type=MESH)

    for partner in partners:
        pl.semaphore_signal(barrier, inc=1, device_id=partner, device_id_type=MESH)

    def rows_of(c):
        return pl.ds(chunks[c][0] * HD, len(chunks[c]) * HD)

    def load(which, c):
        src, dst = ((k_hbm, k_s), (v_hbm, v_s), (q_hbm, q_s))[which]
        cols = rows_of(c)
        return pltpu.make_async_copy(src.at[0, :, cols], dst.at[:, cols], load_sem.at[which, c])

    for c in order[:LEAD]:
        load(0, c).start()
        load(1, c).start()

    @pl.when(is_last)
    def _():
        for c in late:
            load(2, c).start()

    small = [
        pltpu.make_async_copy(src, dst, small_sem.at[i])
        for i, (src, dst) in enumerate(
            ((at_hbm, at_ref), (table_hbm, table_ref), (gain_hbm, gain_ref))
        )
    ]
    for copy in small:
        copy.start()

    def holds(b):
        return lax.rem(me // 2**b, 2) == 1

    def all_below(b):
        return lax.rem(me, 2**b) == 2**b - 1

    def starts(b):
        return has_next & (lax.rem(me, 2 ** (b + 1)) == 2**b - 1)

    def passes(b):
        return holds(b) & jnp.logical_not(all_below(b))

    def up(b, c):
        return pltpu.make_async_remote_copy(
            src_ref=state.at[rows_of(c)], dst_ref=buckets.at[b, rows_of(c)],
            send_sem=up_send.at[c], recv_sem=recv_sem.at[b, c],
            device_id=following, device_id_type=MESH,
        )

    def onward(b, c):
        return pltpu.make_async_remote_copy(
            src_ref=buckets.at[b, rows_of(c)], dst_ref=buckets.at[b, rows_of(c)],
            send_sem=pass_send.at[b, c], recv_sem=recv_sem.at[b, c],
            device_id=following, device_id_type=MESH,
        )

    def per_head(c, body):
        for h in chunks[c]:
            body(h)

    def cols_of(h):
        return pl.ds(h * HD, HD)

    def make_state(h):
        cols = cols_of(h)
        one = dot(k_s[:half, cols], v_s[:half, cols], ROWS_ROWS)
        two = dot(k_s[half:, cols], v_s[half:, cols], ROWS_ROWS)
        first[cols, :] = one.astype(jnp.bfloat16)
        state[cols, :] = (one + two).astype(jnp.bfloat16)

    def ask(what, c):
        src, dst = ((q_s, ask_q), (near_s, ask_near))[what]
        return pltpu.make_async_remote_copy(
            src_ref=src.at[:, rows_of(c)], dst_ref=dst.at[:, rows_of(c)],
            send_sem=ask_send.at[what, c], recv_sem=ask_recv.at[what, c],
            device_id=before, device_id_type=MESH,
        )

    for i, c in enumerate(order):
        load(0, c).wait()
        load(1, c).wait()
        if i + LEAD < count:
            load(0, order[i + LEAD]).start()
            load(1, order[i + LEAD]).start()
        per_head(c, make_state)
        if i == 0:
            pl.semaphore_wait(barrier, n_head)

            @pl.when(is_last)
            def _():
                for d in late:
                    load(2, d).wait()
                    ask(0, d).start()

        @pl.when(starts(0) & jnp.logical_not(helps) if c in late else starts(0))
        def _():
            up(0, c).start()

    @pl.when(has_next)
    def _():
        for c in late:
            load(2, c).start()

    for c in order[: count - LATE]:
        load(2, c).start()

    for copy in small:
        copy.wait()
    table_s[...] = jnp.zeros_like(table_s)
    for level in range(levels):
        table_s[:, level * heads : (level + 1) * heads] = table_ref[level]

    def pick_rows(shard):
        places = shard * tokens + lax.broadcasted_iota(jnp.int32, (tokens, points), 0)
        reached = (at_ref[...] <= places).astype(jnp.float32)
        row = jnp.sum(reached, axis=1, keepdims=True) - 1.0
        number = lax.broadcasted_iota(jnp.int32, (tokens, points), 1).astype(jnp.float32)
        picker = (number == row).astype(jnp.float32)
        return dot(picker, table_s[...], precision=HIGH)

    lam_s[...] = pick_rows(me)

    t_of = lax.broadcasted_iota(jnp.int32, (quarter, quarter), 0)
    s_of = lax.broadcasted_iota(jnp.int32, (quarter, quarter), 1)
    own_span = (t_of // span == s_of // span) & (s_of <= t_of)
    other_span = t_of // span > s_of // span

    def lam_columns(h):
        return [lam_s[:, level * heads + h : level * heads + h + 1] for level in range(levels)]

    def near(h):
        cols = cols_of(h)
        lam = lam_columns(h)
        for i in range(2):
            here = slice(i * half, (i + 1) * half)
            scores = dot(q_s[here, cols], k_s[here, cols], COLS_COLS)
            blocks = []
            for j in range(2):
                rows = slice(j * quarter, (j + 1) * quarter)
                tok = slice(i * half + j * quarter, i * half + (j + 1) * quarter)
                weight = jnp.where(own_span, lam[0][tok], jnp.where(other_span, lam[1][tok], 0.0))
                diagonal = (scores[rows, rows] * weight).astype(jnp.bfloat16)
                if j == 0:
                    side = jnp.zeros((quarter, quarter), jnp.bfloat16)
                    blocks.append(jnp.concatenate([diagonal, side], axis=1))
                else:
                    side = (scores[rows, :quarter] * lam[2][tok]).astype(jnp.bfloat16)
                    blocks.append(jnp.concatenate([side, diagonal], axis=1))
            total = dot(jnp.concatenate(blocks, axis=0), v_s[here, cols])
            if i == 1:
                total += lam[3][here] * dot(q_s[here, cols], first[cols, :])
            mixed[here, cols] = total

    for d, c in enumerate(order):
        for b in range(1, bits):

            @pl.when(starts(b))
            def _():
                total = state[rows_of(c), :].astype(jnp.float32)
                for k in range(b):
                    onward(k, c).wait_recv()
                    total += buckets[k, rows_of(c), :].astype(jnp.float32)
                state[rows_of(c), :] = total.astype(jnp.bfloat16)
                up(b, c).start()

        if d in late:

            @pl.when(has_next)
            def _():
                load(2, d).wait()

            per_head(d, near)

            @pl.when(is_last)
            def _():
                near_s[:, rows_of(d)] = mixed[:, rows_of(d)].astype(jnp.bfloat16)
                ask(1, d).start()

        else:
            load(2, d).wait()
            per_head(d, near)
        for b in range(1, bits):

            @pl.when(passes(b))
            def _():
                onward(b, c).wait_recv()

            @pl.when(passes(b) & jnp.logical_not(helps) if c in late else passes(b))
            def _():
                onward(b, c).start()

    def far(b):
        def body(h):
            cols = cols_of(h)
            lam = lam_columns(h)[LOCAL_BITS + 1 + b]
            mixed[:, cols] += lam * dot(q_s[:, cols], buckets[b, cols, :])

        return body

    def add_squares(h):
        values = mixed[:, cols_of(h)]
        square_s[...] += values * values

    def far_all(chosen, square):
        for b in range(bits):
            for c in chosen:

                @pl.when(holds(b))
                def _():
                    @pl.when(is_last)
                    def _():
                        onward(b, c).wait_recv()

                    per_head(c, far(b))

                if b == bits - 1 and square:
                    per_head(c, add_squares)

    def as_row(squares):
        own = jnp.sum(squares, axis=1, keepdims=True)
        return jnp.transpose(jnp.broadcast_to(own, (tokens, LANES)))[:8]

    def reply():
        return pltpu.make_async_remote_copy(
            src_ref=reply_s, dst_ref=reply_in, send_sem=reply_send, recv_sem=reply_recv,
            device_id=following, device_id_type=MESH,
        )

    @pl.when(helps)
    def _():
        lam_next[...] = pick_rows(me + 1)
        squares = jnp.zeros((tokens, LANES), jnp.float32)
        for c in late:
            ask(0, c).wait_recv()
            ask(1, c).wait_recv()
            for h in chunks[c]:
                cols = cols_of(h)
                values = ask_near[:, cols].astype(jnp.float32)
                for b in range(bits):
                    at = (LOCAL_BITS + 1 + b) * heads + h
                    there = state[cols, :] if b == 0 else buckets[b, cols, :]
                    values += lam_next[:, at : at + 1] * dot(ask_q[:, cols], there)
                squares += values * values
        reply_s[...] = as_row(squares)
        reply().start()
        for c in late:
            up(0, c).start()
        for b in range(1, bits):
            for c in late:
                onward(b, c).start()

    square_s[...] = jnp.zeros_like(square_s)
    far_all(order[: count - LATE], True)

    @pl.when(has_next)
    def _():
        far_all(late, True)

    part_s[...] = as_row(square_s[...])

    @pl.when(is_last)
    def _():
        reply().wait_recv()
        part_s[...] += reply_in[...]

    copies = [
        pltpu.make_async_remote_copy(
            src_ref=part_s, dst_ref=parts_in.at[j], send_sem=part_send.at[j], recv_sem=part_recv.at[j],
            device_id=partner, device_id_type=MESH,
        )
        for j, partner in enumerate(partners)
    ]
    for copy in copies:
        copy.start()

    def weigh(chosen):
        for c in chosen:
            mixed[:, rows_of(c)] = mixed[:, rows_of(c)] * gain_ref[:, rows_of(c)]

    weigh(order[: count - LATE])

    @pl.when(is_last)
    def _():
        far_all(late, False)

    weigh(late)
    total = part_s[...]
    for j, copy in enumerate(copies):
        copy.wait()
        total += parts_in[j]
    scale = lax.rsqrt(total / (HEADS * HD) + EPSILON)
    scale_ref[...] = jnp.transpose(jnp.broadcast_to(scale[:1], (LANES, tokens)))

    for c in range(count):

        @pl.when(has_next)
        def _():
            up(0, c).wait_send()

        for b in range(1, bits):

            @pl.when(passes(b))
            def _():
                onward(b, c).wait_send()

    @pl.when(helps)
    def _():
        reply().wait_send()

    @pl.when(is_last)
    def _():
        for c in late:
            for what in range(2):
                ask(what, c).wait_send()


def finish_kernel(mixed, scale_ref, out_hbm, out_s, store_sem):
    pieces = store_sem.shape[0]
    rows = mixed.shape[0] // pieces

    def store(i):
        here = pl.ds(i * rows, rows)
        return pltpu.make_async_copy(out_s.at[here], out_hbm.at[0, here], store_sem.at[i])

    for i in range(pieces):
        here = pl.ds(i * rows, rows)
        scale = scale_ref[here]
        for h in range(mixed.shape[1] // HD):
            cols = pl.ds(h * HD, HD)
            out_s[here, cols] = (mixed[here, cols] * scale).astype(jnp.bfloat16)
        store(i).start()
    for i in range(pieces):
        store(i).wait()


def on_device(n_seq, n_head, query_rows, key_rows, value_rows, coef_at, coef_table, out_gain):
    batch, tokens, width = query_rows.shape
    points, levels, heads = coef_table.shape
    bits = levels - LOCAL_BITS - 1
    bf16, f32 = jnp.bfloat16, jnp.float32
    dma = pltpu.SemaphoreType.DMA
    count = len(chunk_heads(heads))
    in_vmem = pl.BlockSpec(memory_space=pltpu.VMEM)
    in_hbm = pl.BlockSpec(memory_space=pl.ANY)
    mixed, scale = pl.pallas_call(
        functools.partial(kernel, n_seq, n_head),
        out_shape=(pltpu.VMEM((tokens, width), f32), pltpu.VMEM((tokens, LANES), f32)),
        in_specs=[in_hbm] * 6,
        out_specs=(in_vmem, in_vmem),
        scratch_shapes=[
            pltpu.VMEM((tokens, width), bf16),
            pltpu.VMEM((tokens, width), bf16),
            pltpu.VMEM((tokens, width), bf16),
            pltpu.VMEM((1, points), jnp.int32),
            pltpu.VMEM((levels, points, heads), f32),
            pltpu.VMEM((1, width), f32),
            pltpu.VMEM((width, HD), bf16),
            pltpu.VMEM((width, HD), bf16),
            pltpu.VMEM((bits, width, HD), bf16),
            pltpu.VMEM((points, LANES), f32),
            pltpu.VMEM((tokens, LANES), f32),
            pltpu.VMEM((tokens, LANES), f32),
            pltpu.VMEM((8, tokens), f32),
            pltpu.VMEM((n_head - 1, 8, tokens), f32),
            pltpu.VMEM((tokens, LATE * HD), bf16),
            pltpu.VMEM((tokens, LATE * HD), bf16),
            pltpu.VMEM((tokens, LATE * HD), bf16),
            pltpu.VMEM((tokens, LANES), f32),
            pltpu.VMEM((8, tokens), f32),
            pltpu.VMEM((8, tokens), f32),
            dma((3, count)),
            dma((3,)),
            dma((count,)),
            dma((bits, count)),
            dma((bits, count)),
            dma((n_head - 1,)),
            dma((n_head - 1,)),
            dma((2, LATE)),
            dma((2, LATE)),
            dma(()),
            dma(()),
        ],
        compiler_params=pltpu.CompilerParams(
            collective_id=0, has_side_effects=True, vmem_limit_bytes=56 * 2**20
        ),
    )(query_rows, key_rows, value_rows, coef_at.reshape(1, -1), coef_table.transpose(1, 0, 2), out_gain.reshape(1, -1))
    return pl.pallas_call(
        finish_kernel,
        out_shape=jax.ShapeDtypeStruct((batch, tokens, width), bf16),
        in_specs=[in_vmem] * 2,
        out_specs=in_hbm,
        scratch_shapes=[pltpu.VMEM((tokens, width), bf16), dma((PIECES,))],
        compiler_params=pltpu.CompilerParams(vmem_limit_bytes=8 * 2**20),
    )(mixed, scale)


def solution(mesh):
    placed = (
        P(("groups", "batch"), "seq", "head"),
        P(("groups", "batch"), "seq", "head"),
        P(("groups", "batch"), "seq", "head"),
        P("groups"),
        P("groups", None, "head"),
        P("head"),
    )
    return jax.shard_map(
        functools.partial(on_device, mesh.shape["seq"], mesh.shape["head"]),
        mesh=mesh,
        in_specs=placed,
        out_specs=P(("groups", "batch"), "seq", "head"),
        check_vma=False,
    )
```

```python
import functools

import jax
import jax.numpy as jnp
from jax import lax
from jax.experimental import pallas as pl
from jax.experimental.pallas import tpu as pltpu
from jax.sharding import PartitionSpec as P

HEADS = 32
HD = 128
LOCAL_BITS = 3
EPSILON = 1e-06
HIGH = lax.Precision.HIGHEST
MESH = pl.DeviceIdType.MESH
LANES = 128
LEAD = 3
PIECES = 8
LATE = 3
LATE_ODD = 2
PASSED = {4: 2, 6: 3, 8: 4, 10: 5}
THEN = {0: 6, 3: 7, 4: 8, 5: 9}


ROWS_ROWS = (((0,), (0,)), ((), ()))
COLS_COLS = (((1,), (1,)), ((), ()))


def chunk_heads(heads):
    rest = heads - LATE
    pairs = (rest - 4) // 2
    sizes = [1] * LATE + [1, 1] + [2] * pairs + [1] * (rest - 2 - 2 * pairs)
    return [range(sum(sizes[:c]), sum(sizes[: c + 1])) for c in range(len(sizes))]


def dot(a, b, dims=(((1,), (0,)), ((), ())), precision=None):
    return lax.dot_general(a, b, dims, preferred_element_type=jnp.float32, precision=precision)


def kernel(
    n_seq, n_head,
    q_hbm, k_hbm, v_hbm, at_hbm, table_hbm, gain_hbm, mixed, scale_ref,
    q_s, k_s, v_s, at_ref, table_ref, gain_ref, state, first, buckets, table_s, lam_s, square_s, part_s, parts_in,
    near_s, ask_q, ask_near, lam_next, reply_squares, reply_s, reply_in,
    load_sem, small_sem, up_send, pass_send, recv_sem, part_send, part_recv,
    ask_send, ask_recv, reply_send, reply_recv,
):
    tokens, width = q_s.shape
    levels, heads = table_ref.shape[0], table_ref.shape[2]
    bits = levels - LOCAL_BITS - 1
    points = at_ref.shape[1]
    chunks = chunk_heads(heads)
    count = len(chunks)
    half, quarter = tokens // 2, tokens // 4
    span = tokens // 2**LOCAL_BITS
    me = lax.axis_index("seq")
    hx = lax.axis_index("head")
    has_next = me < n_seq - 1
    is_last = me == n_seq - 1
    helps = me == n_seq - 2
    following = {"seq": lax.rem(me + 1, n_seq)}
    before = {"seq": lax.rem(me + n_seq - 1, n_seq)}
    even = lax.rem(lax.axis_index("batch"), 2) == 0
    late = range(LATE)
    normal = list(range(LATE, count))
    order = [*normal, *late]
    partners = [{"head": lax.rem(hx + j, n_head)} for j in range(1, n_head)]

    barrier = pltpu.get_barrier_semaphore()

    @pl.when(me > 0)
    def _():
        pl.semaphore_signal(barrier, inc=1, device_id=before, device_id_type=MESH)

    @pl.when(helps)
    def _():
        pl.semaphore_signal(barrier, inc=1, device_id=following, device_id_type=MESH)

    for partner in partners:
        pl.semaphore_signal(barrier, inc=1, device_id=partner, device_id_type=MESH)

    def rows_of(c):
        return pl.ds(chunks[c][0] * HD, len(chunks[c]) * HD)

    def load(which, c):
        src, dst = ((k_hbm, k_s), (v_hbm, v_s), (q_hbm, q_s))[which]
        cols = rows_of(c)
        return pltpu.make_async_copy(src.at[0, :, cols], dst.at[:, cols], load_sem.at[which, c])

    for c in order[:LEAD]:
        load(0, c).start()
        load(1, c).start()

    @pl.when(is_last)
    def _():
        for c in late:
            load(2, c).start()

    small = [
        pltpu.make_async_copy(src, dst, small_sem.at[i])
        for i, (src, dst) in enumerate(
            ((at_hbm, at_ref), (table_hbm, table_ref), (gain_hbm, gain_ref))
        )
    ]
    for copy in small:
        copy.start()

    def holds(b):
        return lax.rem(me // 2**b, 2) == 1

    def all_below(b):
        return lax.rem(me, 2**b) == 2**b - 1

    def starts(b):
        return has_next & (lax.rem(me, 2 ** (b + 1)) == 2**b - 1)

    def passes(b):
        return holds(b) & jnp.logical_not(all_below(b))

    def up(b, c):
        return pltpu.make_async_remote_copy(
            src_ref=state.at[rows_of(c)], dst_ref=buckets.at[b, rows_of(c)],
            send_sem=up_send.at[c], recv_sem=recv_sem.at[b, c],
            device_id=following, device_id_type=MESH,
        )

    def onward(b, c):
        return pltpu.make_async_remote_copy(
            src_ref=buckets.at[b, rows_of(c)], dst_ref=buckets.at[b, rows_of(c)],
            send_sem=pass_send.at[b, c], recv_sem=recv_sem.at[b, c],
            device_id=following, device_id_type=MESH,
        )

    def is_late(c):
        return even if c >= LATE_ODD else even == even

    def holds_back(c):
        return helps & is_late(c) if c in late else me < 0

    def asks(c):
        return is_last & is_late(c)

    def carry(b, c):
        @pl.when(starts(b))
        def _():
            total = state[rows_of(c), :].astype(jnp.float32)
            for k in range(b):
                onward(k, c).wait_recv()
                total += buckets[k, rows_of(c), :].astype(jnp.float32)
            state[rows_of(c), :] = total.astype(jnp.bfloat16)
            up(b, c).start()

    def hand_on(b, c):
        @pl.when(passes(b))
        def _():
            onward(b, c).wait_recv()

        @pl.when(passes(b) & jnp.logical_not(holds_back(c)) if c in late else passes(b))
        def _():
            onward(b, c).start()

    def per_head(c, body):
        for h in chunks[c]:
            body(h)

    def cols_of(h):
        return pl.ds(h * HD, HD)

    def make_state(h):
        cols = cols_of(h)
        one = dot(k_s[:half, cols], v_s[:half, cols], ROWS_ROWS)
        two = dot(k_s[half:, cols], v_s[half:, cols], ROWS_ROWS)
        first[cols, :] = one.astype(jnp.bfloat16)
        state[cols, :] = (one + two).astype(jnp.bfloat16)

    def ask(what, c):
        src, dst = ((q_s, ask_q), (near_s, ask_near))[what]
        return pltpu.make_async_remote_copy(
            src_ref=src.at[:, rows_of(c)], dst_ref=dst.at[:, rows_of(c)],
            send_sem=ask_send.at[what, c], recv_sem=ask_recv.at[what, c],
            device_id=before, device_id_type=MESH,
        )

    for i, c in enumerate(order):
        load(0, c).wait()
        load(1, c).wait()
        if i + LEAD < count:
            load(0, order[i + LEAD]).start()
            load(1, order[i + LEAD]).start()
        per_head(c, make_state)
        if i == 0:
            pl.semaphore_wait(barrier, n_head)

            @pl.when(is_last)
            def _():
                for d in late:
                    load(2, d).wait()

            for d in late:

                @pl.when(asks(d))
                def _():
                    ask(0, d).start()

        @pl.when(starts(0) & jnp.logical_not(holds_back(c)) if c in late else starts(0))
        def _():
            up(0, c).start()


    @pl.when(has_next)
    def _():
        for c in late:
            load(2, c).start()

    for c in normal:
        load(2, c).start()

    for copy in small:
        copy.wait()
    table_s[...] = jnp.zeros_like(table_s)
    for level in range(levels):
        table_s[:, level * heads : (level + 1) * heads] = table_ref[level]

    def pick_rows(shard):
        places = shard * tokens + lax.broadcasted_iota(jnp.int32, (tokens, points), 0)
        reached = (at_ref[...] <= places).astype(jnp.float32)
        row = jnp.sum(reached, axis=1, keepdims=True) - 1.0
        number = lax.broadcasted_iota(jnp.int32, (tokens, points), 1).astype(jnp.float32)
        picker = (number == row).astype(jnp.float32)
        return dot(picker, table_s[...], precision=HIGH)

    lam_s[...] = pick_rows(me)

    t_of = lax.broadcasted_iota(jnp.int32, (quarter, quarter), 0)
    s_of = lax.broadcasted_iota(jnp.int32, (quarter, quarter), 1)
    own_span = (t_of // span == s_of // span) & (s_of <= t_of)
    other_span = t_of // span > s_of // span

    def lam_columns(h):
        return [lam_s[:, level * heads + h : level * heads + h + 1] for level in range(levels)]

    def near(h):
        cols = cols_of(h)
        lam = lam_columns(h)
        for i in range(2):
            here = slice(i * half, (i + 1) * half)
            scores = dot(q_s[here, cols], k_s[here, cols], COLS_COLS)
            blocks = []
            for j in range(2):
                rows = slice(j * quarter, (j + 1) * quarter)
                tok = slice(i * half + j * quarter, i * half + (j + 1) * quarter)
                weight = jnp.where(own_span, lam[0][tok], jnp.where(other_span, lam[1][tok], 0.0))
                diagonal = (scores[rows, rows] * weight).astype(jnp.bfloat16)
                if j == 0:
                    side = jnp.zeros((quarter, quarter), jnp.bfloat16)
                    blocks.append(jnp.concatenate([diagonal, side], axis=1))
                else:
                    side = (scores[rows, :quarter] * lam[2][tok]).astype(jnp.bfloat16)
                    blocks.append(jnp.concatenate([side, diagonal], axis=1))
            total = dot(jnp.concatenate(blocks, axis=0), v_s[here, cols])
            if i == 1:
                total += lam[3][here] * dot(q_s[here, cols], first[cols, :])
            mixed[here, cols] = total

    passed = 0
    for d, c in enumerate(order):
        for b in range(1, bits):
            carry(b, c)

        if d in late:

            @pl.when(has_next)
            def _():
                load(2, d).wait()

            per_head(d, near)

            @pl.when(asks(d))
            def _():
                near_s[:, rows_of(d)] = mixed[:, rows_of(d)].astype(jnp.bfloat16)
                ask(1, d).start()

        else:
            load(2, d).wait()
            per_head(d, near)
        for e in order[PASSED.get(d - 1, passed) : PASSED.get(d, passed)]:
            for b in range(1, bits):
                hand_on(b, e)
        passed = PASSED.get(d, passed)

    def far(b, weighed=False):
        def body(h):
            cols = cols_of(h)
            lam = lam_columns(h)[LOCAL_BITS + 1 + b]
            total = mixed[:, cols] + lam * dot(q_s[:, cols], buckets[b, cols, :])
            mixed[:, cols] = total * gain_ref[:, cols] if weighed else total

        return body

    def add_squares(h):
        values = mixed[:, cols_of(h)]
        square_s[...] += values * values

    def far_of(b, c):
        @pl.when(holds(b))
        def _():
            @pl.when(is_last)
            def _():
                onward(b, c).wait_recv()

            per_head(c, far(b))

        if b == bits - 1:
            per_head(c, add_squares)

    def far_late(b, c):
        @pl.when(asks(c))
        def _():
            onward(b, c).wait_recv()
            per_head(c, far(b, b == bits - 1))

    def as_row(squares):
        own = jnp.sum(squares, axis=1, keepdims=True)
        return jnp.transpose(jnp.broadcast_to(own, (tokens, LANES)))[:8]

    def reply():
        return pltpu.make_async_remote_copy(
            src_ref=reply_s, dst_ref=reply_in, send_sem=reply_send, recv_sem=reply_recv,
            device_id=following, device_id_type=MESH,
        )

    @pl.when(helps)
    def _():
        lam_next[...] = pick_rows(me + 1)

    def help_next(c):
        @pl.when(helps & is_late(c))
        def _():
            ask(0, c).wait_recv()
            ask(1, c).wait_recv()
            for h in chunks[c]:
                cols = cols_of(h)
                values = ask_near[:, cols].astype(jnp.float32)
                for b in range(bits):
                    at = (LOCAL_BITS + 1 + b) * heads + h
                    there = state[cols, :] if b == 0 else buckets[b, cols, :]
                    values += lam_next[:, at : at + 1] * dot(ask_q[:, cols], there)
                if c == 0:
                    reply_squares[...] = values * values
                else:
                    reply_squares[...] += values * values

    def send_late():
        reply_s[...] = as_row(reply_squares[...])
        reply().start()
        for b in range(bits):
            for c in late:

                @pl.when(is_late(c))
                def _():
                    (onward(b, c) if b else up(b, c)).start()

    square_s[...] = jnp.zeros_like(square_s)
    for b in range(bits):
        done = passed
        for i, c in enumerate(order):
            ahead = max(THEN.get(i, 0), i + 1, done)
            for e in order[done:ahead] if b > 0 else ():
                hand_on(b, e)
            done = ahead
            if b == bits - 1 and c in late:
                help_next(c)
                if c == late[-1]:
                    pl.when(helps)(send_late)
            if c in late:

                @pl.when(jnp.logical_not(asks(c)))
                def _():
                    far_of(b, c)

            else:
                far_of(b, c)

    part_s[...] = as_row(square_s[...])

    @pl.when(is_last)
    def _():
        reply().wait_recv()
        part_s[...] += reply_in[...]

    copies = [
        pltpu.make_async_remote_copy(
            src_ref=part_s, dst_ref=parts_in.at[j], send_sem=part_send.at[j], recv_sem=part_recv.at[j],
            device_id=partner, device_id_type=MESH,
        )
        for j, partner in enumerate(partners)
    ]
    for copy in copies:
        copy.start()

    def weigh(h):
        mixed[:, cols_of(h)] = mixed[:, cols_of(h)] * gain_ref[:, cols_of(h)]

    for c in order:
        if c in late:

            @pl.when(jnp.logical_not(asks(c)))
            def _():
                per_head(c, weigh)

        else:
            per_head(c, weigh)

    for b in range(bits):
        for c in late if b < bits - 1 else late[:-1]:
            far_late(b, c)

    total = part_s[...]
    for j, copy in enumerate(copies):
        copy.wait()
        total += parts_in[j]
    scale = lax.rsqrt(total / (HEADS * HD) + EPSILON)
    scale_ref[...] = jnp.transpose(jnp.broadcast_to(scale[:1], (LANES, tokens)))
    far_late(bits - 1, late[-1])

    for c in range(count):

        @pl.when(has_next)
        def _():
            up(0, c).wait_send()

        for b in range(1, bits):

            @pl.when(passes(b))
            def _():
                onward(b, c).wait_send()

    @pl.when(helps)
    def _():
        reply().wait_send()

    @pl.when(is_last)
    def _():
        for c in late:

            @pl.when(is_late(c))
            def _():
                for what in range(2):
                    ask(what, c).wait_send()


def finish_kernel(mixed, scale_ref, out_hbm, out_s, store_sem):
    pieces = store_sem.shape[0]
    rows = mixed.shape[0] // pieces

    def store(i):
        here = pl.ds(i * rows, rows)
        return pltpu.make_async_copy(out_s.at[here], out_hbm.at[0, here], store_sem.at[i])

    for i in range(pieces):
        here = pl.ds(i * rows, rows)
        scale = scale_ref[here]
        for h in range(mixed.shape[1] // HD):
            cols = pl.ds(h * HD, HD)
            out_s[here, cols] = (mixed[here, cols] * scale).astype(jnp.bfloat16)
        store(i).start()
    for i in range(pieces):
        store(i).wait()


def on_device(n_seq, n_head, query_rows, key_rows, value_rows, coef_at, coef_table, out_gain):
    batch, tokens, width = query_rows.shape
    points, levels, heads = coef_table.shape
    bits = levels - LOCAL_BITS - 1
    bf16, f32 = jnp.bfloat16, jnp.float32
    dma = pltpu.SemaphoreType.DMA
    count = len(chunk_heads(heads))
    in_vmem = pl.BlockSpec(memory_space=pltpu.VMEM)
    in_hbm = pl.BlockSpec(memory_space=pl.ANY)
    mixed, scale = pl.pallas_call(
        functools.partial(kernel, n_seq, n_head),
        out_shape=(pltpu.VMEM((tokens, width), f32), pltpu.VMEM((tokens, LANES), f32)),
        in_specs=[in_hbm] * 6,
        out_specs=(in_vmem, in_vmem),
        scratch_shapes=[
            pltpu.VMEM((tokens, width), bf16),
            pltpu.VMEM((tokens, width), bf16),
            pltpu.VMEM((tokens, width), bf16),
            pltpu.VMEM((1, points), jnp.int32),
            pltpu.VMEM((levels, points, heads), f32),
            pltpu.VMEM((1, width), f32),
            pltpu.VMEM((width, HD), bf16),
            pltpu.VMEM((width, HD), bf16),
            pltpu.VMEM((bits, width, HD), bf16),
            pltpu.VMEM((points, LANES), f32),
            pltpu.VMEM((tokens, LANES), f32),
            pltpu.VMEM((tokens, LANES), f32),
            pltpu.VMEM((8, tokens), f32),
            pltpu.VMEM((n_head - 1, 8, tokens), f32),
            pltpu.VMEM((tokens, LATE * HD), bf16),
            pltpu.VMEM((tokens, LATE * HD), bf16),
            pltpu.VMEM((tokens, LATE * HD), bf16),
            pltpu.VMEM((tokens, LANES), f32),
            pltpu.VMEM((tokens, LANES), f32),
            pltpu.VMEM((8, tokens), f32),
            pltpu.VMEM((8, tokens), f32),
            dma((3, count)),
            dma((3,)),
            dma((count,)),
            dma((bits, count)),
            dma((bits, count)),
            dma((n_head - 1,)),
            dma((n_head - 1,)),
            dma((2, LATE)),
            dma((2, LATE)),
            dma(()),
            dma(()),
        ],
        compiler_params=pltpu.CompilerParams(
            collective_id=0, has_side_effects=True, vmem_limit_bytes=56 * 2**20
        ),
    )(query_rows, key_rows, value_rows, coef_at.reshape(1, -1), coef_table.transpose(1, 0, 2), out_gain.reshape(1, -1))
    return pl.pallas_call(
        finish_kernel,
        out_shape=jax.ShapeDtypeStruct((batch, tokens, width), bf16),
        in_specs=[in_vmem] * 2,
        out_specs=in_hbm,
        scratch_shapes=[pltpu.VMEM((tokens, width), bf16), dma((PIECES,))],
        compiler_params=pltpu.CompilerParams(vmem_limit_bytes=8 * 2**20),
    )(mixed, scale)


def solution(mesh):
    placed = (
        P(("groups", "batch"), "seq", "head"),
        P(("groups", "batch"), "seq", "head"),
        P(("groups", "batch"), "seq", "head"),
        P("groups"),
        P("groups", None, "head"),
        P("head"),
    )
    return jax.shard_map(
        functools.partial(on_device, mesh.shape["seq"], mesh.shape["head"]),
        mesh=mesh,
        in_specs=placed,
        out_specs=P(("groups", "batch"), "seq", "head"),
        check_vma=False,
    )
```

```python
import functools

import jax
import jax.numpy as jnp
from jax import lax
from jax.experimental import pallas as pl
from jax.experimental.pallas import tpu as pltpu
from jax.sharding import PartitionSpec as P

HEADS = 32
HD = 128
LOCAL_BITS = 3
EPSILON = 1e-06
HIGH = lax.Precision.HIGHEST
MESH = pl.DeviceIdType.MESH
LANES = 128
LEAD = 3
EDGES = (0, 1, 3, 7, 12, 17, 22, 27, 32)
LATE = 3
LATE_ODD = 2
PASSED = {4: 2, 6: 3, 8: 4, 10: 5}
THEN = {0: 6, 3: 7, 4: 8, 5: 9}


ROWS_ROWS = (((0,), (0,)), ((), ()))
COLS_COLS = (((1,), (1,)), ((), ()))


def chunk_heads(heads):
    rest = heads - LATE
    pairs = (rest - 4) // 2
    sizes = [1] * LATE + [1, 1] + [2] * pairs + [1] * (rest - 2 - 2 * pairs)
    return [range(sum(sizes[:c]), sum(sizes[: c + 1])) for c in range(len(sizes))]


def dot(a, b, dims=(((1,), (0,)), ((), ())), precision=None):
    return lax.dot_general(a, b, dims, preferred_element_type=jnp.float32, precision=precision)


def kernel(
    n_seq, n_head,
    q_hbm, k_hbm, v_hbm, at_hbm, table_hbm, gain_hbm, mixed, scale_ref, gain_ref,
    q_s, k_s, v_s, at_ref, table_ref, state, first, buckets, table_s, lam_s, square_s, part_s, parts_in,
    near_s, ask_q, ask_near, lam_next, reply_squares, reply_s, reply_in,
    load_sem, small_sem, up_send, pass_send, recv_sem, part_send, part_recv,
    ask_send, ask_recv, reply_send, reply_recv,
):
    tokens, width = q_s.shape
    levels, heads = table_ref.shape[0], table_ref.shape[2]
    bits = levels - LOCAL_BITS - 1
    points = at_ref.shape[1]
    chunks = chunk_heads(heads)
    count = len(chunks)
    half, quarter = tokens // 2, tokens // 4
    span = tokens // 2**LOCAL_BITS
    me = lax.axis_index("seq")
    hx = lax.axis_index("head")
    has_next = me < n_seq - 1
    is_last = me == n_seq - 1
    helps = me == n_seq - 2
    following = {"seq": lax.rem(me + 1, n_seq)}
    before = {"seq": lax.rem(me + n_seq - 1, n_seq)}
    even = lax.rem(lax.axis_index("batch"), 2) == 0
    late = range(LATE)
    normal = list(range(LATE, count))
    order = [*normal, *late]
    partners = [{"head": lax.rem(hx + j, n_head)} for j in range(1, n_head)]

    barrier = pltpu.get_barrier_semaphore()

    @pl.when(me > 0)
    def _():
        pl.semaphore_signal(barrier, inc=1, device_id=before, device_id_type=MESH)

    @pl.when(helps)
    def _():
        pl.semaphore_signal(barrier, inc=1, device_id=following, device_id_type=MESH)

    for partner in partners:
        pl.semaphore_signal(barrier, inc=1, device_id=partner, device_id_type=MESH)

    def rows_of(c):
        return pl.ds(chunks[c][0] * HD, len(chunks[c]) * HD)

    def load(which, c):
        src, dst = ((k_hbm, k_s), (v_hbm, v_s), (q_hbm, q_s))[which]
        cols = rows_of(c)
        return pltpu.make_async_copy(src.at[0, :, cols], dst.at[:, cols], load_sem.at[which, c])

    for c in order[:LEAD]:
        load(0, c).start()
        load(1, c).start()

    @pl.when(is_last)
    def _():
        for c in late:
            load(2, c).start()

    small = [
        pltpu.make_async_copy(src, dst, small_sem.at[i])
        for i, (src, dst) in enumerate(
            ((at_hbm, at_ref), (table_hbm, table_ref), (gain_hbm, gain_ref))
        )
    ]
    for copy in small:
        copy.start()

    def holds(b):
        return lax.rem(me // 2**b, 2) == 1

    def all_below(b):
        return lax.rem(me, 2**b) == 2**b - 1

    def starts(b):
        return has_next & (lax.rem(me, 2 ** (b + 1)) == 2**b - 1)

    def passes(b):
        return holds(b) & jnp.logical_not(all_below(b))

    def up(b, c):
        return pltpu.make_async_remote_copy(
            src_ref=state.at[rows_of(c)], dst_ref=buckets.at[b, rows_of(c)],
            send_sem=up_send.at[c], recv_sem=recv_sem.at[b, c],
            device_id=following, device_id_type=MESH,
        )

    def onward(b, c):
        return pltpu.make_async_remote_copy(
            src_ref=buckets.at[b, rows_of(c)], dst_ref=buckets.at[b, rows_of(c)],
            send_sem=pass_send.at[b, c], recv_sem=recv_sem.at[b, c],
            device_id=following, device_id_type=MESH,
        )

    def is_late(c):
        return even if c >= LATE_ODD else even == even

    def holds_back(c):
        return helps & is_late(c) if c in late else me < 0

    def asks(c):
        return is_last & is_late(c)

    def carry(b, c):
        @pl.when(starts(b))
        def _():
            total = state[rows_of(c), :].astype(jnp.float32)
            for k in range(b):
                onward(k, c).wait_recv()
                total += buckets[k, rows_of(c), :].astype(jnp.float32)
            state[rows_of(c), :] = total.astype(jnp.bfloat16)
            up(b, c).start()

    def hand_on(b, c):
        @pl.when(passes(b))
        def _():
            onward(b, c).wait_recv()

        @pl.when(passes(b) & jnp.logical_not(holds_back(c)) if c in late else passes(b))
        def _():
            onward(b, c).start()

    def per_head(c, body):
        for h in chunks[c]:
            body(h)

    def cols_of(h):
        return pl.ds(h * HD, HD)

    def make_state(h):
        cols = cols_of(h)
        one = dot(k_s[:half, cols], v_s[:half, cols], ROWS_ROWS)
        two = dot(k_s[half:, cols], v_s[half:, cols], ROWS_ROWS)
        first[cols, :] = one.astype(jnp.bfloat16)
        state[cols, :] = (one + two).astype(jnp.bfloat16)

    def ask(what, c):
        src, dst = ((q_s, ask_q), (near_s, ask_near))[what]
        return pltpu.make_async_remote_copy(
            src_ref=src.at[:, rows_of(c)], dst_ref=dst.at[:, rows_of(c)],
            send_sem=ask_send.at[what, c], recv_sem=ask_recv.at[what, c],
            device_id=before, device_id_type=MESH,
        )

    for i, c in enumerate(order):
        load(0, c).wait()
        load(1, c).wait()
        if i + LEAD < count:
            load(0, order[i + LEAD]).start()
            load(1, order[i + LEAD]).start()
        per_head(c, make_state)
        if i == 0:
            pl.semaphore_wait(barrier, n_head)

            @pl.when(is_last)
            def _():
                for d in late:
                    load(2, d).wait()

            for d in late:

                @pl.when(asks(d))
                def _():
                    ask(0, d).start()

        @pl.when(starts(0) & jnp.logical_not(holds_back(c)) if c in late else starts(0))
        def _():
            up(0, c).start()


    @pl.when(has_next)
    def _():
        for c in late:
            load(2, c).start()

    for c in normal:
        load(2, c).start()

    for copy in small:
        copy.wait()
    table_s[...] = jnp.zeros_like(table_s)
    for level in range(levels):
        table_s[:, level * heads : (level + 1) * heads] = table_ref[level]

    def pick_rows(shard):
        places = shard * tokens + lax.broadcasted_iota(jnp.int32, (tokens, points), 0)
        reached = (at_ref[...] <= places).astype(jnp.float32)
        row = jnp.sum(reached, axis=1, keepdims=True) - 1.0
        number = lax.broadcasted_iota(jnp.int32, (tokens, points), 1).astype(jnp.float32)
        picker = (number == row).astype(jnp.float32)
        return dot(picker, table_s[...], precision=HIGH)

    lam_s[...] = pick_rows(me)

    t_of = lax.broadcasted_iota(jnp.int32, (quarter, quarter), 0)
    s_of = lax.broadcasted_iota(jnp.int32, (quarter, quarter), 1)
    own_span = (t_of // span == s_of // span) & (s_of <= t_of)
    other_span = t_of // span > s_of // span

    def lam_columns(h):
        return [lam_s[:, level * heads + h : level * heads + h + 1] for level in range(levels)]

    def near(h):
        cols = cols_of(h)
        lam = lam_columns(h)
        for i in range(2):
            here = slice(i * half, (i + 1) * half)
            scores = dot(q_s[here, cols], k_s[here, cols], COLS_COLS)
            blocks = []
            for j in range(2):
                rows = slice(j * quarter, (j + 1) * quarter)
                tok = slice(i * half + j * quarter, i * half + (j + 1) * quarter)
                weight = jnp.where(own_span, lam[0][tok], jnp.where(other_span, lam[1][tok], 0.0))
                diagonal = (scores[rows, rows] * weight).astype(jnp.bfloat16)
                if j == 0:
                    side = jnp.zeros((quarter, quarter), jnp.bfloat16)
                    blocks.append(jnp.concatenate([diagonal, side], axis=1))
                else:
                    side = (scores[rows, :quarter] * lam[2][tok]).astype(jnp.bfloat16)
                    blocks.append(jnp.concatenate([side, diagonal], axis=1))
            total = dot(jnp.concatenate(blocks, axis=0), v_s[here, cols])
            if i == 1:
                total += lam[3][here] * dot(q_s[here, cols], first[cols, :])
            mixed[here, cols] = total

    passed = 0
    for d, c in enumerate(order):
        for b in range(1, bits):
            carry(b, c)

        if d in late:

            @pl.when(has_next)
            def _():
                load(2, d).wait()

            per_head(d, near)

            @pl.when(asks(d))
            def _():
                near_s[:, rows_of(d)] = mixed[:, rows_of(d)].astype(jnp.bfloat16)
                ask(1, d).start()

        else:
            load(2, d).wait()
            per_head(d, near)
        for e in order[PASSED.get(d - 1, passed) : PASSED.get(d, passed)]:
            for b in range(1, bits):
                hand_on(b, e)
        passed = PASSED.get(d, passed)

    def far(b):
        def body(h):
            cols = cols_of(h)
            lam = lam_columns(h)[LOCAL_BITS + 1 + b]
            mixed[:, cols] += lam * dot(q_s[:, cols], buckets[b, cols, :])

        return body

    def add_squares(h):
        values = mixed[:, cols_of(h)]
        square_s[...] += values * values

    def far_of(b, c):
        @pl.when(holds(b))
        def _():
            @pl.when(is_last)
            def _():
                onward(b, c).wait_recv()

            per_head(c, far(b))

        if b == bits - 1:
            per_head(c, add_squares)

    def far_late(b, c):
        @pl.when(asks(c))
        def _():
            onward(b, c).wait_recv()
            per_head(c, far(b))

    def as_row(squares):
        own = jnp.sum(squares, axis=1, keepdims=True)
        return jnp.transpose(jnp.broadcast_to(own, (tokens, LANES)))[:8]

    def reply():
        return pltpu.make_async_remote_copy(
            src_ref=reply_s, dst_ref=reply_in, send_sem=reply_send, recv_sem=reply_recv,
            device_id=following, device_id_type=MESH,
        )

    @pl.when(helps)
    def _():
        lam_next[...] = pick_rows(me + 1)

    def help_next(c):
        @pl.when(helps & is_late(c))
        def _():
            ask(0, c).wait_recv()
            ask(1, c).wait_recv()
            for h in chunks[c]:
                cols = cols_of(h)
                values = ask_near[:, cols].astype(jnp.float32)
                for b in range(bits):
                    at = (LOCAL_BITS + 1 + b) * heads + h
                    there = state[cols, :] if b == 0 else buckets[b, cols, :]
                    values += lam_next[:, at : at + 1] * dot(ask_q[:, cols], there)
                if c == 0:
                    reply_squares[...] = values * values
                else:
                    reply_squares[...] += values * values

    def send_late():
        reply_s[...] = as_row(reply_squares[...])
        reply().start()
        for b in range(bits):
            for c in late:

                @pl.when(is_late(c))
                def _():
                    (onward(b, c) if b else up(b, c)).start()

    square_s[...] = jnp.zeros_like(square_s)
    for b in range(bits):
        done = passed
        for i, c in enumerate(order):
            ahead = max(THEN.get(i, 0), i + 1, done)
            for e in order[done:ahead] if b > 0 else ():
                hand_on(b, e)
            done = ahead
            if b == bits - 1 and c in late:
                help_next(c)
                if c == late[-1]:
                    pl.when(helps)(send_late)
            if c in late:

                @pl.when(jnp.logical_not(asks(c)))
                def _():
                    far_of(b, c)

            else:
                far_of(b, c)

    part_s[...] = as_row(square_s[...])

    @pl.when(is_last)
    def _():
        reply().wait_recv()
        part_s[...] += reply_in[...]

    copies = [
        pltpu.make_async_remote_copy(
            src_ref=part_s, dst_ref=parts_in.at[j], send_sem=part_send.at[j], recv_sem=part_recv.at[j],
            device_id=partner, device_id_type=MESH,
        )
        for j, partner in enumerate(partners)
    ]
    for copy in copies:
        copy.start()

    for b in range(bits):
        for c in late if b < bits - 1 else late[:-1]:
            far_late(b, c)

    total = part_s[...]
    for j, copy in enumerate(copies):
        copy.wait()
        total += parts_in[j]
    scale = lax.rsqrt(total / (HEADS * HD) + EPSILON)
    scale_ref[...] = jnp.transpose(jnp.broadcast_to(scale[:1], (LANES, tokens)))
    far_late(bits - 1, late[-1])

    for c in range(count):

        @pl.when(has_next)
        def _():
            up(0, c).wait_send()

        for b in range(1, bits):

            @pl.when(passes(b))
            def _():
                onward(b, c).wait_send()

    @pl.when(helps)
    def _():
        reply().wait_send()

    @pl.when(is_last)
    def _():
        for c in late:

            @pl.when(is_late(c))
            def _():
                for what in range(2):
                    ask(what, c).wait_send()


def finish_kernel(mixed, scale_ref, gain_ref, out_hbm, out_s, store_sem):
    tokens, width = mixed.shape
    edges = [tokens * part // 32 for part in EDGES]
    blocks = [pl.ds(here, after - here) for here, after in zip(edges, edges[1:])]

    def store(i):
        return pltpu.make_async_copy(out_s.at[blocks[i]], out_hbm.at[0, blocks[i]], store_sem.at[i])

    for i, here in enumerate(blocks):
        scale = scale_ref[here]
        for h in range(width // HD):
            cols = pl.ds(h * HD, HD)
            out_s[here, cols] = (mixed[here, cols] * scale * gain_ref[:, cols]).astype(jnp.bfloat16)
        store(i).start()
    for i in range(len(blocks)):
        store(i).wait()


def on_device(n_seq, n_head, query_rows, key_rows, value_rows, coef_at, coef_table, out_gain):
    batch, tokens, width = query_rows.shape
    points, levels, heads = coef_table.shape
    bits = levels - LOCAL_BITS - 1
    bf16, f32 = jnp.bfloat16, jnp.float32
    dma = pltpu.SemaphoreType.DMA
    count = len(chunk_heads(heads))
    in_vmem = pl.BlockSpec(memory_space=pltpu.VMEM)
    in_hbm = pl.BlockSpec(memory_space=pl.ANY)
    mixed, scale, gain = pl.pallas_call(
        functools.partial(kernel, n_seq, n_head),
        out_shape=(pltpu.VMEM((tokens, width), f32), pltpu.VMEM((tokens, LANES), f32), pltpu.VMEM((1, width), f32)),
        in_specs=[in_hbm] * 6,
        out_specs=(in_vmem, in_vmem, in_vmem),
        scratch_shapes=[
            pltpu.VMEM((tokens, width), bf16),
            pltpu.VMEM((tokens, width), bf16),
            pltpu.VMEM((tokens, width), bf16),
            pltpu.VMEM((1, points), jnp.int32),
            pltpu.VMEM((levels, points, heads), f32),
            pltpu.VMEM((width, HD), bf16),
            pltpu.VMEM((width, HD), bf16),
            pltpu.VMEM((bits, width, HD), bf16),
            pltpu.VMEM((points, LANES), f32),
            pltpu.VMEM((tokens, LANES), f32),
            pltpu.VMEM((tokens, LANES), f32),
            pltpu.VMEM((8, tokens), f32),
            pltpu.VMEM((n_head - 1, 8, tokens), f32),
            pltpu.VMEM((tokens, LATE * HD), bf16),
            pltpu.VMEM((tokens, LATE * HD), bf16),
            pltpu.VMEM((tokens, LATE * HD), bf16),
            pltpu.VMEM((tokens, LANES), f32),
            pltpu.VMEM((tokens, LANES), f32),
            pltpu.VMEM((8, tokens), f32),
            pltpu.VMEM((8, tokens), f32),
            dma((3, count)),
            dma((3,)),
            dma((count,)),
            dma((bits, count)),
            dma((bits, count)),
            dma((n_head - 1,)),
            dma((n_head - 1,)),
            dma((2, LATE)),
            dma((2, LATE)),
            dma(()),
            dma(()),
        ],
        compiler_params=pltpu.CompilerParams(
            collective_id=0, has_side_effects=True, vmem_limit_bytes=56 * 2**20
        ),
    )(query_rows, key_rows, value_rows, coef_at.reshape(1, -1), coef_table.transpose(1, 0, 2), out_gain.reshape(1, -1))
    return pl.pallas_call(
        finish_kernel,
        out_shape=jax.ShapeDtypeStruct((batch, tokens, width), bf16),
        in_specs=[in_vmem] * 3,
        out_specs=in_hbm,
        scratch_shapes=[pltpu.VMEM((tokens, width), bf16), dma((len(EDGES) - 1,))],
        compiler_params=pltpu.CompilerParams(vmem_limit_bytes=8 * 2**20),
    )(mixed, scale, gain)


def solution(mesh):
    placed = (
        P(("groups", "batch"), "seq", "head"),
        P(("groups", "batch"), "seq", "head"),
        P(("groups", "batch"), "seq", "head"),
        P("groups"),
        P("groups", None, "head"),
        P("head"),
    )
    return jax.shard_map(
        functools.partial(on_device, mesh.shape["seq"], mesh.shape["head"]),
        mesh=mesh,
        in_specs=placed,
        out_specs=P(("groups", "batch"), "seq", "head"),
        check_vma=False,
    )
```

```python
import functools

import jax
import jax.numpy as jnp
from jax import lax
from jax.experimental import pallas as pl
from jax.experimental.pallas import tpu as pltpu
from jax.sharding import PartitionSpec as P

HEADS = 32
HD = 128
LOCAL_BITS = 3
EPSILON = 1e-06
HIGH = lax.Precision.HIGHEST
MESH = pl.DeviceIdType.MESH
LANES = 128
LEAD = 3
EDGES = (0, 1, 3, 7, 12, 17, 22, 27, 32)
LATE = 3
LATE_ODD = 2
PASSED = {4: 2, 6: 3, 8: 4, 10: 5}
THEN = {0: 6, 3: 7, 4: 8, 5: 9}


ROWS_ROWS = (((0,), (0,)), ((), ()))
COLS_COLS = (((1,), (1,)), ((), ()))


def chunk_heads(heads):
    rest = heads - LATE
    pairs = (rest - 4) // 2
    sizes = [1] * LATE + [1, 1] + [2] * pairs + [1] * (rest - 2 - 2 * pairs)
    return [range(sum(sizes[:c]), sum(sizes[: c + 1])) for c in range(len(sizes))]


def dot(a, b, dims=(((1,), (0,)), ((), ())), precision=None):
    return lax.dot_general(a, b, dims, preferred_element_type=jnp.float32, precision=precision)


def kernel(
    n_seq, n_head,
    q_hbm, k_hbm, v_hbm, at_hbm, table_hbm, gain_hbm, mixed, scale_ref, gain_ref,
    q_s, k_s, v_s, at_ref, table_ref, state, first, buckets, table_s, lam_s, square_s, part_s, parts_in,
    near_s, ask_q, ask_near, lam_next, reply_squares, reply_s, reply_in,
    load_sem, small_sem, up_send, pass_send, recv_sem, part_send, part_recv,
    ask_send, ask_recv, reply_send, reply_recv,
):
    tokens, width = q_s.shape
    levels, heads = table_ref.shape[0], table_ref.shape[2]
    bits = levels - LOCAL_BITS - 1
    points = at_ref.shape[1]
    chunks = chunk_heads(heads)
    count = len(chunks)
    half, quarter = tokens // 2, tokens // 4
    span = tokens // 2**LOCAL_BITS
    me = lax.axis_index("seq")
    hx = lax.axis_index("head")
    has_next = me < n_seq - 1
    is_last = me == n_seq - 1
    helps = me == n_seq - 2
    following = {"seq": lax.rem(me + 1, n_seq)}
    before = {"seq": lax.rem(me + n_seq - 1, n_seq)}
    even = lax.rem(lax.axis_index("batch"), 2) == 0
    late = range(LATE)
    normal = list(range(LATE, count))
    order = [*normal, *late]
    partners = [{"head": lax.rem(hx + j, n_head)} for j in range(1, n_head)]

    barrier = pltpu.get_barrier_semaphore()

    @pl.when(me > 0)
    def _():
        pl.semaphore_signal(barrier, inc=1, device_id=before, device_id_type=MESH)

    @pl.when(helps)
    def _():
        pl.semaphore_signal(barrier, inc=1, device_id=following, device_id_type=MESH)

    for partner in partners:
        pl.semaphore_signal(barrier, inc=1, device_id=partner, device_id_type=MESH)

    def rows_of(c):
        return pl.ds(chunks[c][0] * HD, len(chunks[c]) * HD)

    def load(which, c):
        src, dst = ((k_hbm, k_s), (v_hbm, v_s), (q_hbm, q_s))[which]
        cols = rows_of(c)
        return pltpu.make_async_copy(src.at[0, :, cols], dst.at[:, cols], load_sem.at[which, c])

    for c in order[:LEAD]:
        load(0, c).start()
        load(1, c).start()

    @pl.when(is_last)
    def _():
        for c in late:
            load(2, c).start()

    small = [
        pltpu.make_async_copy(src, dst, small_sem.at[i])
        for i, (src, dst) in enumerate(
            ((at_hbm, at_ref), (table_hbm, table_ref), (gain_hbm, gain_ref))
        )
    ]
    for copy in small:
        copy.start()

    def holds(b):
        return lax.rem(me // 2**b, 2) == 1

    def all_below(b):
        return lax.rem(me, 2**b) == 2**b - 1

    def starts(b):
        return has_next & (lax.rem(me, 2 ** (b + 1)) == 2**b - 1)

    def passes(b):
        return holds(b) & jnp.logical_not(all_below(b))

    def up(b, c):
        return pltpu.make_async_remote_copy(
            src_ref=state.at[rows_of(c)], dst_ref=buckets.at[b, rows_of(c)],
            send_sem=up_send.at[c], recv_sem=recv_sem.at[b, c],
            device_id=following, device_id_type=MESH,
        )

    def onward(b, c):
        return pltpu.make_async_remote_copy(
            src_ref=buckets.at[b, rows_of(c)], dst_ref=buckets.at[b, rows_of(c)],
            send_sem=pass_send.at[b, c], recv_sem=recv_sem.at[b, c],
            device_id=following, device_id_type=MESH,
        )

    def is_late(c):
        return even if c >= LATE_ODD else even == even

    def holds_back(c):
        return helps & is_late(c) if c in late else me < 0

    def asks(c):
        return is_last & is_late(c)

    def carry(b, c):
        @pl.when(starts(b))
        def _():
            total = state[rows_of(c), :].astype(jnp.float32)
            for k in range(b):
                onward(k, c).wait_recv()
                total += buckets[k, rows_of(c), :].astype(jnp.float32)
            state[rows_of(c), :] = total.astype(jnp.bfloat16)
            up(b, c).start()

    def hand_on(b, c):
        @pl.when(passes(b))
        def _():
            onward(b, c).wait_recv()

        @pl.when(passes(b) & jnp.logical_not(holds_back(c)) if c in late else passes(b))
        def _():
            onward(b, c).start()

    def per_head(c, body):
        for h in chunks[c]:
            body(h)

    def cols_of(h):
        return pl.ds(h * HD, HD)

    def make_state(h):
        cols = cols_of(h)
        one = dot(k_s[:half, cols], v_s[:half, cols], ROWS_ROWS)
        two = dot(k_s[half:, cols], v_s[half:, cols], ROWS_ROWS)
        first[cols, :] = one.astype(jnp.bfloat16)
        state[cols, :] = (one + two).astype(jnp.bfloat16)

    def ask(what, c):
        src, dst = ((q_s, ask_q), (near_s, ask_near))[what]
        return pltpu.make_async_remote_copy(
            src_ref=src.at[:, rows_of(c)], dst_ref=dst.at[:, rows_of(c)],
            send_sem=ask_send.at[what, c], recv_sem=ask_recv.at[what, c],
            device_id=before, device_id_type=MESH,
        )

    for i, c in enumerate(order):
        load(0, c).wait()
        load(1, c).wait()
        if i + LEAD < count:
            load(0, order[i + LEAD]).start()
            load(1, order[i + LEAD]).start()
        per_head(c, make_state)
        if i == 0:
            pl.semaphore_wait(barrier, n_head)

            @pl.when(is_last)
            def _():
                for d in late:
                    load(2, d).wait()

            for d in late:

                @pl.when(asks(d))
                def _():
                    ask(0, d).start()

        @pl.when(starts(0) & jnp.logical_not(holds_back(c)) if c in late else starts(0))
        def _():
            up(0, c).start()


    @pl.when(has_next)
    def _():
        for c in late:
            load(2, c).start()

    for c in normal:
        load(2, c).start()

    for copy in small:
        copy.wait()
    table_s[...] = jnp.zeros_like(table_s)
    for level in range(levels):
        table_s[:, level * heads : (level + 1) * heads] = table_ref[level]

    def pick_rows(shard):
        places = shard * tokens + lax.broadcasted_iota(jnp.int32, (tokens, points), 0)
        reached = (at_ref[...] <= places).astype(jnp.float32)
        row = jnp.sum(reached, axis=1, keepdims=True) - 1.0
        number = lax.broadcasted_iota(jnp.int32, (tokens, points), 1).astype(jnp.float32)
        picker = (number == row).astype(jnp.float32)
        return dot(picker, table_s[...], precision=HIGH)

    lam_s[...] = pick_rows(me)

    t_of = lax.broadcasted_iota(jnp.int32, (quarter, quarter), 0)
    s_of = lax.broadcasted_iota(jnp.int32, (quarter, quarter), 1)
    own_span = (t_of // span == s_of // span) & (s_of <= t_of)
    other_span = t_of // span > s_of // span

    def lam_columns(h):
        return [lam_s[:, level * heads + h : level * heads + h + 1] for level in range(levels)]

    def near(h):
        cols = cols_of(h)
        lam = lam_columns(h)
        for i in range(2):
            here = slice(i * half, (i + 1) * half)
            scores = dot(q_s[here, cols], k_s[here, cols], COLS_COLS)
            blocks = []
            for j in range(2):
                rows = slice(j * quarter, (j + 1) * quarter)
                tok = slice(i * half + j * quarter, i * half + (j + 1) * quarter)
                weight = jnp.where(own_span, lam[0][tok], jnp.where(other_span, lam[1][tok], 0.0))
                diagonal = (scores[rows, rows] * weight).astype(jnp.bfloat16)
                if j == 0:
                    side = jnp.zeros((quarter, quarter), jnp.bfloat16)
                    blocks.append(jnp.concatenate([diagonal, side], axis=1))
                else:
                    side = (scores[rows, :quarter] * lam[2][tok]).astype(jnp.bfloat16)
                    blocks.append(jnp.concatenate([side, diagonal], axis=1))
            total = dot(jnp.concatenate(blocks, axis=0), v_s[here, cols])
            if i == 1:
                total += lam[3][here] * dot(q_s[here, cols], first[cols, :])
            mixed[here, cols] = total

    passed = 0
    for d, c in enumerate(order):
        for b in range(1, bits):
            carry(b, c)

        if d in late:

            @pl.when(has_next)
            def _():
                load(2, d).wait()

            per_head(d, near)

            @pl.when(asks(d))
            def _():
                near_s[:, rows_of(d)] = mixed[:, rows_of(d)].astype(jnp.bfloat16)
                ask(1, d).start()

        else:
            load(2, d).wait()
            per_head(d, near)
        for e in order[PASSED.get(d - 1, passed) : PASSED.get(d, passed)]:
            for b in range(1, bits):
                hand_on(b, e)
        passed = PASSED.get(d, passed)

    def far(b):
        def body(h):
            cols = cols_of(h)
            lam = lam_columns(h)[LOCAL_BITS + 1 + b]
            mixed[:, cols] += lam * dot(q_s[:, cols], buckets[b, cols, :])

        return body

    def add_squares(h):
        values = mixed[:, cols_of(h)]
        square_s[...] += values * values

    def far_of(b, c):
        @pl.when(holds(b))
        def _():
            @pl.when(is_last)
            def _():
                onward(b, c).wait_recv()

            per_head(c, far(b))

        if b == bits - 1:
            per_head(c, add_squares)

    def far_late(b, c):
        @pl.when(asks(c))
        def _():
            onward(b, c).wait_recv()
            per_head(c, far(b))

    def as_row(squares):
        own = jnp.sum(squares, axis=1, keepdims=True)
        return jnp.transpose(jnp.broadcast_to(own, (tokens, LANES)))[:8]

    def reply():
        return pltpu.make_async_remote_copy(
            src_ref=reply_s, dst_ref=reply_in, send_sem=reply_send, recv_sem=reply_recv,
            device_id=following, device_id_type=MESH,
        )

    @pl.when(helps)
    def _():
        lam_next[...] = pick_rows(me + 1)

    def help_next(c):
        @pl.when(helps & is_late(c))
        def _():
            ask(0, c).wait_recv()
            ask(1, c).wait_recv()
            for h in chunks[c]:
                cols = cols_of(h)
                values = ask_near[:, cols].astype(jnp.float32)
                for b in range(bits):
                    at = (LOCAL_BITS + 1 + b) * heads + h
                    there = state[cols, :] if b == 0 else buckets[b, cols, :]
                    values += lam_next[:, at : at + 1] * dot(ask_q[:, cols], there)
                if c == 0:
                    reply_squares[...] = values * values
                else:
                    reply_squares[...] += values * values

    def send_late():
        reply_s[...] = as_row(reply_squares[...])
        reply().start()
        for b in range(bits):
            for c in late:

                @pl.when(is_late(c))
                def _():
                    (onward(b, c) if b else up(b, c)).start()

    square_s[...] = jnp.zeros_like(square_s)
    for b in range(bits):
        done = passed
        for i, c in enumerate(order):
            ahead = max(THEN.get(i, 0), i + 1, done)
            for e in order[done:ahead] if b > 0 else ():
                hand_on(b, e)
            done = ahead
            if b == bits - 1 and c in late:
                help_next(c)
                if c == late[-1]:
                    pl.when(helps)(send_late)
            if c in late:

                @pl.when(jnp.logical_not(asks(c)))
                def _():
                    far_of(b, c)

            else:
                far_of(b, c)

    part_s[...] = as_row(square_s[...])

    @pl.when(is_last)
    def _():
        reply().wait_recv()
        part_s[...] += reply_in[...]

    copies = [
        pltpu.make_async_remote_copy(
            src_ref=part_s, dst_ref=parts_in.at[j], send_sem=part_send.at[j], recv_sem=part_recv.at[j],
            device_id=partner, device_id_type=MESH,
        )
        for j, partner in enumerate(partners)
    ]
    for copy in copies:
        copy.start()

    for b in range(bits):
        for c in late if b < bits - 1 else late[:-1]:
            far_late(b, c)

    @pl.when(hx == 0)
    def _():
        far_late(bits - 1, late[-1])

    total = part_s[...]
    for j, copy in enumerate(copies):
        copy.wait_recv()
        total += parts_in[j]
    scale = lax.rsqrt(total / (HEADS * HD) + EPSILON)
    scale_ref[...] = jnp.transpose(jnp.broadcast_to(scale[:1], (LANES, tokens)))

    @pl.when(hx > 0)
    def _():
        far_late(bits - 1, late[-1])

    for copy in copies:
        copy.wait_send()
    for c in range(count):

        @pl.when(has_next)
        def _():
            up(0, c).wait_send()

        for b in range(1, bits):

            @pl.when(passes(b))
            def _():
                onward(b, c).wait_send()

    @pl.when(helps)
    def _():
        reply().wait_send()

    @pl.when(is_last)
    def _():
        for c in late:

            @pl.when(is_late(c))
            def _():
                for what in range(2):
                    ask(what, c).wait_send()


def finish_kernel(mixed, scale_ref, gain_ref, out_hbm, out_s, store_sem):
    tokens, width = mixed.shape
    edges = [tokens * part // 32 for part in EDGES]
    blocks = [pl.ds(here, after - here) for here, after in zip(edges, edges[1:])]

    def store(i):
        return pltpu.make_async_copy(out_s.at[blocks[i]], out_hbm.at[0, blocks[i]], store_sem.at[i])

    for i, here in enumerate(blocks):
        scale = scale_ref[here]
        for h in range(width // HD):
            cols = pl.ds(h * HD, HD)
            out_s[here, cols] = (mixed[here, cols] * scale * gain_ref[:, cols]).astype(jnp.bfloat16)
        store(i).start()
    for i in range(len(blocks)):
        store(i).wait()


def on_device(n_seq, n_head, query_rows, key_rows, value_rows, coef_at, coef_table, out_gain):
    batch, tokens, width = query_rows.shape
    points, levels, heads = coef_table.shape
    bits = levels - LOCAL_BITS - 1
    bf16, f32 = jnp.bfloat16, jnp.float32
    dma = pltpu.SemaphoreType.DMA
    count = len(chunk_heads(heads))
    in_vmem = pl.BlockSpec(memory_space=pltpu.VMEM)
    in_hbm = pl.BlockSpec(memory_space=pl.ANY)
    mixed, scale, gain = pl.pallas_call(
        functools.partial(kernel, n_seq, n_head),
        out_shape=(pltpu.VMEM((tokens, width), f32), pltpu.VMEM((tokens, LANES), f32), pltpu.VMEM((1, width), f32)),
        in_specs=[in_hbm] * 6,
        out_specs=(in_vmem, in_vmem, in_vmem),
        scratch_shapes=[
            pltpu.VMEM((tokens, width), bf16),
            pltpu.VMEM((tokens, width), bf16),
            pltpu.VMEM((tokens, width), bf16),
            pltpu.VMEM((1, points), jnp.int32),
            pltpu.VMEM((levels, points, heads), f32),
            pltpu.VMEM((width, HD), bf16),
            pltpu.VMEM((width, HD), bf16),
            pltpu.VMEM((bits, width, HD), bf16),
            pltpu.VMEM((points, LANES), f32),
            pltpu.VMEM((tokens, LANES), f32),
            pltpu.VMEM((tokens, LANES), f32),
            pltpu.VMEM((8, tokens), f32),
            pltpu.VMEM((n_head - 1, 8, tokens), f32),
            pltpu.VMEM((tokens, LATE * HD), bf16),
            pltpu.VMEM((tokens, LATE * HD), bf16),
            pltpu.VMEM((tokens, LATE * HD), bf16),
            pltpu.VMEM((tokens, LANES), f32),
            pltpu.VMEM((tokens, LANES), f32),
            pltpu.VMEM((8, tokens), f32),
            pltpu.VMEM((8, tokens), f32),
            dma((3, count)),
            dma((3,)),
            dma((count,)),
            dma((bits, count)),
            dma((bits, count)),
            dma((n_head - 1,)),
            dma((n_head - 1,)),
            dma((2, LATE)),
            dma((2, LATE)),
            dma(()),
            dma(()),
        ],
        compiler_params=pltpu.CompilerParams(
            collective_id=0, has_side_effects=True, vmem_limit_bytes=56 * 2**20
        ),
    )(query_rows, key_rows, value_rows, coef_at.reshape(1, -1), coef_table.transpose(1, 0, 2), out_gain.reshape(1, -1))
    return pl.pallas_call(
        finish_kernel,
        out_shape=jax.ShapeDtypeStruct((batch, tokens, width), bf16),
        in_specs=[in_vmem] * 3,
        out_specs=in_hbm,
        scratch_shapes=[pltpu.VMEM((tokens, width), bf16), dma((len(EDGES) - 1,))],
        compiler_params=pltpu.CompilerParams(vmem_limit_bytes=8 * 2**20),
    )(mixed, scale, gain)


def solution(mesh):
    placed = (
        P(("groups", "batch"), "seq", "head"),
        P(("groups", "batch"), "seq", "head"),
        P(("groups", "batch"), "seq", "head"),
        P("groups"),
        P("groups", None, "head"),
        P("head"),
    )
    return jax.shard_map(
        functools.partial(on_device, mesh.shape["seq"], mesh.shape["head"]),
        mesh=mesh,
        in_specs=placed,
        out_specs=P(("groups", "batch"), "seq", "head"),
        check_vma=False,
    )
```
